32 devices in a mesh: row: 4 (over y, x), col: 8 (over z, core).
Axes of the slice: x: 2, y: 2, z: 4, core: 2. Of those that a mesh axis runs over, the one named last changes fastest.
Arguments:
- tokens: bfloat16 [4096, 2048], P(('row', 'col')), may hold values from -6 to 6
- cotangent: bfloat16 [4096, 2048], P(('row', 'col')), may hold values from -6 to 6
- permutation: int32 [4096], replicated, may hold values from 0 to 4095, as said below
- lengths: int32 [8, 4], P('col'), may hold values from 1 to 384, 512 in all within a row
- attention_gain: bfloat16 [2048], replicated, may hold values from 0.5 to 1.5
- query_projection_weight: bfloat16 [2048, 2048], P('col', 'row'), may hold values from -0.125 to 0.125
- key_value_weight: bfloat16 [2048, 512], P('col'), may hold values from -0.125 to 0.125
- projection_adapter_first: bfloat16 [2048, 256], P('col'), may hold values from -0.125 to 0.125
- query_adapter_second: bfloat16 [256, 2048], P(None, 'row'), may hold values from -0.375 to 0.375
- key_value_second: bfloat16 [256, 512], replicated, may hold values from -0.375 to 0.375
- output_projection_weight: bfloat16 [2048, 2048], P('row', 'col'), may hold values from -2 to 2
- output_adapter_first: bfloat16 [2048, 256], P('row'), may hold values from -2 to 2
- output_adapter_second: bfloat16 [256, 2048], replicated, may hold values from -0.375 to 0.375
- hidden_gain: bfloat16 [2048], replicated, may hold values from 0.5 to 1.5
- gate_up_weight: bfloat16 [2048, 2, 16384], P('col', None, 'row'), may hold values from -0.125 to 0.125
- widen_adapter_first: bfloat16 [2048, 256], P('col'), may hold values from -0.125 to 0.125
- widen_adapter_second: bfloat16 [256, 2, 16384], P(None, None, 'row'), may hold values from -0.375 to 0.375
- down_projection_weight: bfloat16 [16384, 2048], P('row', 'col'), may hold values from -0.046875 to 0.046875
- narrow_adapter_first: bfloat16 [16384, 256], P('row'), may hold values from -0.046875 to 0.046875
- narrow_adapter_second: bfloat16 [256, 2048], replicated, may hold values from -0.375 to 0.375
Outputs:
- block_output: bfloat16 [4096, 2048], P(('row', 'col'))
- grad_tokens: bfloat16 [4096, 2048], P(('row', 'col'))
- grad_attention_gain: float32 [2048], replicated
- grad_query_weight: float32 [2048, 2048], P('col', 'row')
- grad_keyval_weight: float32 [2048, 512], P('col')
- projection_first_gradient: float32 [2048, 256], P('col')
- query_second_gradient: float32 [256, 2048], P(None, 'row')
- key_value_second_gradient: float32 [256, 512], replicated
- grad_output_weight: float32 [2048, 2048], P('row', 'col')
- output_first_gradient: float32 [2048, 256], P('row')
- output_second_gradient: float32 [256, 2048], replicated
- grad_hidden_gain: float32 [2048], replicated
- grad_expand_weight: float32 [2048, 2, 16384], P('col', None, 'row')
- widen_first_gradient: float32 [2048, 256], P('col')
- widen_second_gradient: float32 [256, 2, 16384], P(None, None, 'row')
- grad_shrink_weight: float32 [16384, 2048], P('row', 'col')
- narrow_first_gradient: float32 [16384, 256], P('row')
- narrow_second_gradient: float32 [256, 2048], replicated
The draws below stay inside these ranges and needn't reach their ends.
Inputs may be any that keep to these rules, and one draw needn't show every extreme that they name: `permutation`: packed position (c * 512) + r * 128 + s, for token group c, row device r and slot s < 128, takes a token from the given positions (r * 8 + s // 16) * 128 to that plus 128 - 1; every given position appears once. `lengths`: each row sums to 512.
All inputs are finite; a program needn't handle non-finite values.
Results may differ from the reference program's by a relative error of at most 0.025.
Values may be sent and summed in bfloat16 or wider, within the bound.
No kernel may reach another device: no remote copies, remote signals or barrier semaphores. Data moves between devices by JAX's collectives and lax.ppermute only.
A program may use at most 320 MiB of HBM per device.

```python
import math
import jax
import jax.numpy as jnp
import numpy as np
from jax import lax

D = 2048
HEADS = 8
HD = 256
FF = 16384
RANK = 256
SEQS = 4
TOK_DEV = 128
GROUP = 512
TOKENS = 4096
SHARE = 16
LONGEST = 384
N_ROW = 4
N_COL = 8


def draw_permutation(key, part):
    device_total = N_ROW * N_COL
    key_list = jax.random.split(key, device_total)
    orders = jax.vmap(lambda one_key: jax.random.permutation(one_key, TOK_DEV))(key_list).reshape(N_ROW, N_COL, TOK_DEV)
    targets = jnp.arange(N_COL, dtype=jnp.int32)[:, None, None, None]
    row_ids = jnp.arange(N_ROW, dtype=jnp.int32)[None, :, None, None]
    source_cols = jnp.arange(N_COL, dtype=jnp.int32)[None, None, :, None]
    slot_ids = jnp.arange(SHARE, dtype=jnp.int32)[None, None, None, :]
    local_slots = orders[row_ids, source_cols, targets * SHARE + slot_ids]
    given = (row_ids * N_COL + source_cols) * TOK_DEV + local_slots
    return given.reshape(-1).astype(jnp.int32)


def block_scale(stream_key, extent, cuts, least, top_value):
    gain, own = 1.0, jax.random.fold_in(stream_key, 6)
    for position, blocks in cuts:
        steps = jnp.exp(jax.random.uniform(jax.random.fold_in(own, position), (blocks,), jnp.float32, least / len(cuts), top_value / len(cuts)))
        gain = gain * jnp.repeat(steps, extent[position] // blocks).reshape([-1 if axis == position else 1 for axis in range(len(extent))])
    return gain


def profile(count, total, most, skew):
    portions = [(1 << 20) // math.isqrt(standing ** skew) + 1 for standing in range(2, count + 1)]
    rest, given = total - most - (count - 1), [1] * (count - 1)
    while rest > 0:
        candidates = [i for i in range(count - 1) if given[i] < most]
        pool, remaining = sum([portions[i] for i in candidates]), rest
        for i in candidates:
            more = min(most - given[i], max(1, remaining * portions[i] // pool), rest)
            given[i] = given[i] + more
            rest = rest - more
    return np.array([most] + given)


def ragged_sizes(key, count, total, bound, lean):
    if count == 2:
        one = jax.random.randint(key, (), max(1, total - bound), min(bound, total - 1) + 1)
        return jnp.stack([one, total - one])
    tallies = jnp.asarray(profile(count, total, bound, lean), jnp.int32)
    pairs = (count - 1) // 2
    giver, taker = tallies[1:1 + 2 * pairs:2], tallies[2:2 + 2 * pairs:2]
    margin = jnp.minimum(giver - 1, bound - taker)
    passed = jax.random.randint(jax.random.fold_in(key, 1), (pairs,), 0, 1 << 20) % (margin + 1)
    tallies = tallies.at[1:1 + 2 * pairs:2].set(giver - passed).at[2:2 + 2 * pairs:2].set(taker + passed)
    return tallies[jax.random.permutation(jax.random.fold_in(key, 2), count)]


def gaussian(own_key, extent, width, limit, shards=(), kind=jnp.bfloat16):
    values = jax.random.normal(own_key, extent, jnp.float32) * width
    if len(shards) > 0:
        values = block_scale(own_key, extent, shards, -0.22, 0.18) * values
    return jnp.clip(values, min=-limit, max=limit).astype(kind)


def setup_inputs(seed: int = 0) -> dict:
    seeds = jax.random.split(jax.random.key(seed), 21)
    return {
        "tokens": gaussian(seeds[0], (TOKENS, D), 1.0, 6.0, ((0, 32),)),
        "cotangent": gaussian(seeds[1], (TOKENS, D), 1.0, 6.0, ((0, 32),)),
        "permutation": draw_permutation(jax.random.fold_in(seeds[20], 71), 0),
        "lengths": jax.vmap(lambda own: ragged_sizes(own, SEQS, GROUP, LONGEST, 2))(jax.random.split(seeds[3], (TOKENS // GROUP))).reshape((TOKENS // GROUP, SEQS)).astype(jnp.int32),
        "attention_gain": jnp.clip(1.0 + 0.1 * jax.random.normal(seeds[4], (D,), jnp.float32), 0.5, 1.5).astype(jnp.bfloat16),
        "query_projection_weight": gaussian(seeds[5], (D, HEADS * HD), D ** -0.5, 0.125, ((0, 8), (1, 4))),
        "key_value_weight": gaussian(seeds[6], (D, 2 * HD), D ** -0.5, 0.125, ((0, 8),)),
        "projection_adapter_first": gaussian(seeds[7], (D, RANK), D ** -0.5, 0.125, ((0, 8),)),
        "query_adapter_second": gaussian(seeds[8], (RANK, HEADS * HD), RANK ** -0.5, 0.375, ((1, 4),)),
        "key_value_second": gaussian(seeds[9], (RANK, 2 * HD), RANK ** -0.5, 0.375),
        "output_projection_weight": gaussian(seeds[10], (HEADS * HD, D), (HEADS * HD // 256) ** -0.5, 2.0, ((0, 4), (1, 8))),
        "output_adapter_first": gaussian(seeds[11], (HEADS * HD, RANK), (HEADS * HD // 256) ** -0.5, 2.0, ((0, 4),)),
        "output_adapter_second": gaussian(seeds[12], (RANK, D), RANK ** -0.5, 0.375),
        "hidden_gain": jnp.clip(1.0 + 0.1 * jax.random.normal(seeds[13], (D,), jnp.float32), 0.5, 1.5).astype(jnp.bfloat16),
        "gate_up_weight": gaussian(seeds[14], (D, 2, FF), D ** -0.5, 0.125, ((0, 8), (2, 4))),
        "widen_adapter_first": gaussian(seeds[15], (D, RANK), D ** -0.5, 0.125, ((0, 8),)),
        "widen_adapter_second": gaussian(seeds[16], (RANK, 2, FF), RANK ** -0.5, 0.375, ((2, 4),)),
        "down_projection_weight": gaussian(seeds[17], (FF, D), FF ** -0.5, 0.046875, ((0, 4), (1, 8))),
        "narrow_adapter_first": gaussian(seeds[18], (FF, RANK), FF ** -0.5, 0.046875, ((0, 4),)),
        "narrow_adapter_second": gaussian(seeds[19], (RANK, D), RANK ** -0.5, 0.375),
    }


EPSILON = 1e-06
MASKED = -1e+30
HIGHEST_PRECISION = lax.Precision.HIGHEST

@jax.custom_vjp
def reduced_rank_rows(v):
    return lax.optimization_barrier(v.astype(jnp.bfloat16)).astype(jnp.float32)

@jax.custom_vjp
def reduced_rank_gradient(v):
    return v

def low_keep(v):
    return (reduced_rank_rows(v), None)

def low_pass(kept, grad):
    return (grad,)

def back_keep(v):
    return (v, None)

def back_low(kept, grad):
    return (reduced_rank_rows(grad),)
reduced_rank_rows.defvjp(low_keep, low_pass)
reduced_rank_gradient.defvjp(back_keep, back_low)

def matrix_product(left_op, right_op):
    return jnp.dot(left_op, right_op, precision=HIGHEST_PRECISION, preferred_element_type=jnp.float32)

def normalize(values, norm_gain):
    inverse = lax.rsqrt(lax.optimization_barrier(jnp.mean(values * values, axis=1, keepdims=True)) + EPSILON)
    return values * inverse * norm_gain

def rotary_tables(positions, head_dim):
    half_dim = head_dim // 2
    inverse_freq = jnp.exp(jnp.arange(half_dim, dtype=jnp.float32) * (-2.0 * math.log(10000.0) / head_dim))
    angles = positions.astype(jnp.float32)[:, None] * inverse_freq[None, :]
    return (jnp.cos(angles), jnp.sin(angles))

def rotate(values, cosine, sine_table):
    half_dim = values.shape[-1] // 2
    first_half = values[..., :half_dim]
    second_half = values[..., half_dim:]
    return jnp.concatenate([first_half * cosine - second_half * sine_table, second_half * cosine + first_half * sine_table], axis=-1)

def group_layout(lengths, group_size):
    seq_ends = jnp.cumsum(lengths, axis=-1).astype(jnp.int32)
    starts = (seq_ends - lengths).astype(jnp.int32)
    places = jnp.arange(group_size, dtype=jnp.int32)
    segment = lax.optimization_barrier(jnp.sum((places[:, None] >= seq_ends[..., None, :]).astype(jnp.int32), axis=-1)).astype(jnp.int32)
    chosen = segment[..., None] == jnp.arange(lengths.shape[-1], dtype=jnp.int32)
    offsets = lax.optimization_barrier(jnp.sum(jnp.where(chosen, starts[..., None, :], 0), axis=-1)).astype(jnp.int32)
    return (segment, (places - offsets).astype(jnp.int32))

def softmax_rows(scores):
    maximum = lax.optimization_barrier(jnp.max(scores, axis=-1, keepdims=True))
    exponent = jnp.exp(scores - maximum)
    return exponent / lax.optimization_barrier(jnp.sum(exponent, axis=-1, keepdims=True))

def group_forward(params, input_rows, segment, positions):
    attention_gain, query_projection_weight, key_value_weight, projection_adapter_first, query_adapter_second, key_value_second, output_projection_weight, output_adapter_first, output_adapter_second, hidden_gain, gate_up_weight, widen_adapter_first, widen_adapter_second, down_projection_weight, narrow_adapter_first, narrow_adapter_second = params
    group_size = input_rows.shape[0]
    head_dim = key_value_weight.shape[1] // 2
    heads_total = query_projection_weight.shape[1] // head_dim
    cosine, sine_table = rotary_tables(positions, head_dim)
    normalized_input = reduced_rank_rows(normalize(input_rows, attention_gain))
    adapter_projection = reduced_rank_rows(reduced_rank_gradient(matrix_product(normalized_input, projection_adapter_first)))
    query_linear = reduced_rank_gradient(matrix_product(normalized_input, query_projection_weight) + matrix_product(adapter_projection, query_adapter_second))
    key_value_linear = reduced_rank_gradient(matrix_product(normalized_input, key_value_weight) + matrix_product(adapter_projection, key_value_second))
    queries = reduced_rank_rows(rotate(query_linear.reshape(group_size, heads_total, head_dim), cosine[:, None, :], sine_table[:, None, :]) * head_dim ** (-0.5))
    key_rows = reduced_rank_rows(rotate(key_value_linear[:, :head_dim], cosine, sine_table))
    value_rows = reduced_rank_rows(key_value_linear[:, head_dim:])
    scores = reduced_rank_gradient(jnp.einsum('qhd,kd->hqk', queries, key_rows, precision=HIGHEST_PRECISION))
    places = jnp.arange(group_size)
    allowed = (segment[:, None] == segment[None, :]) & (places[None, :] <= places[:, None])
    scores = jnp.where(allowed[None], scores, MASKED)
    probs_low = reduced_rank_rows(softmax_rows(scores))
    mixed_values = jnp.einsum('hqk,kd->qhd', probs_low, value_rows, precision=HIGHEST_PRECISION).reshape(group_size, -1)
    mixed_values = reduced_rank_rows(reduced_rank_gradient(mixed_values))
    adapter_output = reduced_rank_rows(reduced_rank_gradient(matrix_product(mixed_values, output_adapter_first)))
    hidden_state = input_rows + reduced_rank_gradient(matrix_product(mixed_values, output_projection_weight) + matrix_product(adapter_output, output_adapter_second))
    normalized_middle = reduced_rank_rows(normalize(hidden_state, hidden_gain))
    adapter_middle = reduced_rank_rows(reduced_rank_gradient(matrix_product(normalized_middle, widen_adapter_first)))
    gate_portion = reduced_rank_gradient(matrix_product(normalized_middle, gate_up_weight[:, 0, :]) + matrix_product(adapter_middle, widen_adapter_second[:, 0, :]))
    up_portion = reduced_rank_gradient(matrix_product(normalized_middle, gate_up_weight[:, 1, :]) + matrix_product(adapter_middle, widen_adapter_second[:, 1, :]))
    activated_hidden = reduced_rank_rows(jax.nn.gelu(gate_portion, approximate=True) * up_portion)
    adapter_final = reduced_rank_rows(reduced_rank_gradient(matrix_product(activated_hidden, narrow_adapter_first)))
    return hidden_state + reduced_rank_gradient(matrix_product(activated_hidden, down_projection_weight) + matrix_product(adapter_final, narrow_adapter_second))

def reference(tokens, cotangent, permutation, lengths, attention_gain, query_projection_weight, key_value_weight, projection_adapter_first, query_adapter_second, key_value_second, output_projection_weight, output_adapter_first, output_adapter_second, hidden_gain, gate_up_weight, widen_adapter_first, widen_adapter_second, down_projection_weight, narrow_adapter_first, narrow_adapter_second):
    params = tuple((argument.astype(jnp.float32) for argument in (attention_gain, query_projection_weight, key_value_weight, projection_adapter_first, query_adapter_second, key_value_second, output_projection_weight, output_adapter_first, output_adapter_second, hidden_gain, gate_up_weight, widen_adapter_first, widen_adapter_second, down_projection_weight, narrow_adapter_first, narrow_adapter_second)))
    hidden_width = tokens.shape[1]
    group_count = lengths.shape[0]
    packed_in = tokens[permutation].astype(jnp.float32).reshape(group_count, -1, hidden_width)
    packed_grad = cotangent[permutation].astype(jnp.float32).reshape(group_count, -1, hidden_width)
    group_size = packed_in.shape[1]
    segment, positions = group_layout(lengths, group_size)

    def forward(weights, input_rows):

        def one_group(pieces):
            return group_forward(weights, pieces[0], pieces[1], pieces[2])
        return lax.map(jax.checkpoint(one_group), (input_rows, segment, positions))
    outputs, pullback = jax.vjp(forward, params, packed_in)
    grad_params, grad_inputs = pullback(packed_grad)
    inverse = jnp.argsort(permutation)
    block_output = outputs.reshape(-1, hidden_width)[inverse].astype(jnp.bfloat16)
    grad_tokens = grad_inputs.reshape(-1, hidden_width)[inverse].astype(jnp.bfloat16)
    return (block_output, grad_tokens, grad_params[0], grad_params[1], grad_params[2], grad_params[3], grad_params[4], grad_params[5], grad_params[6], grad_params[7], grad_params[8], grad_params[9], grad_params[10], grad_params[11], grad_params[12], grad_params[13], grad_params[14], grad_params[15])
```

```python
import math

import jax
import jax.numpy as jnp
from jax import lax
from jax.experimental import pallas as pl
from jax.experimental.pallas import tpu as pltpu
from jax.sharding import PartitionSpec as P


EPSILON = 1e-06
MASKED = -1e30
CORES = 2


def matrix_product(left_op, right_op):
    return jnp.dot(left_op, right_op, preferred_element_type=jnp.float32)


def inner_row_count(left_op, right_op):
    return lax.dot_general(
        left_op, right_op, (((0,), (0,)), ((), ())), preferred_element_type=jnp.float32
    )


def inner_column_count(left_op, right_op):
    return lax.dot_general(
        left_op, right_op, (((1,), (1,)), ((), ())), preferred_element_type=jnp.float32
    )


def normalize(values, norm_gain):
    inverse = lax.rsqrt(jnp.mean(values * values, axis=1, keepdims=True) + EPSILON)
    return values * inverse * norm_gain


def rotary_tables(positions, head_dim):
    half_dim = head_dim // 2
    inverse_freq = jnp.exp(
        jnp.arange(half_dim, dtype=jnp.float32) * (-2.0 * math.log(10000.0) / head_dim)
    )
    angles = positions.astype(jnp.float32)[:, None] * inverse_freq[None, :]
    return (jnp.cos(angles), jnp.sin(angles))


def rotate(values, cosine, sine_table):
    half_dim = values.shape[-1] // 2
    first_half = values[..., :half_dim]
    second_half = values[..., half_dim:]
    return jnp.concatenate(
        [
            first_half * cosine - second_half * sine_table,
            second_half * cosine + first_half * sine_table,
        ],
        axis=-1,
    )


def group_layout(lengths, places):
    seq_ends = jnp.cumsum(lengths, axis=-1)
    starts = seq_ends - lengths
    segment = jnp.sum((places[:, None] >= seq_ends[None, :]).astype(jnp.int32), axis=-1)
    chosen = segment[:, None] == jnp.arange(lengths.shape[0], dtype=jnp.int32)[None, :]
    offsets = jnp.sum(jnp.where(chosen, starts[None, :], 0), axis=-1)
    return (segment, places - offsets)


def low(values):
    return values.astype(jnp.bfloat16)


def wide(values):
    return values.astype(jnp.float32)


def swap_row(values, step):
    return lax.ppermute(values, "row", [(s, s ^ step) for s in range(lax.axis_size("row"))])


def swap_z(values, step):
    return lax.ppermute(
        values, "col", [(s, s ^ (CORES * step)) for s in range(lax.axis_size("col"))]
    )


def swap_core(values):
    return lax.ppermute(values, "col", [(s, s ^ 1) for s in range(lax.axis_size("col"))])


def spread_row(values):
    return [values] + [swap_row(values, d) for d in range(1, lax.axis_size("row"))]


def spread_wide(values):
    if lax.axis_size("row") != 4:
        return spread_row(values)
    size = values.shape[0] // 2
    first = swap_row(values, 1)
    second = swap_row(values, 2)
    corner = jnp.concatenate([swap_row(first[:size], 2), swap_row(second[size:], 1)])
    return [values, first, second, corner]


def absolute(blocks, index):
    bit = 1
    while bit < len(blocks):
        taken = (index & bit) != 0
        blocks = [jnp.where(taken, blocks[i ^ bit], blocks[i]) for i in range(len(blocks))]
        bit *= 2
    return blocks


def spread_z(values):
    found = {0: values}
    step = lax.axis_size("col") // CORES // 2
    while step > 0:
        for d, block in list(found.items()):
            found[d ^ step] = swap_z(block, step)
        step //= 2
    return [found[d] for d in range(len(found))]


def tree_sum(parts):
    while len(parts) > 1:
        parts = [parts[i] + parts[i + 1] for i in range(0, len(parts), 2)]
    return parts[0]


def scatter_row(blocks):
    return tree_sum(
        [wide(blocks[0])]
        + [wide(swap_row(low(b), d)) for d, b in enumerate(blocks) if d > 0]
    )


def scatter_z(blocks):
    return tree_sum(
        [wide(blocks[0])]
        + [wide(swap_z(low(b), d)) for d, b in enumerate(blocks) if d > 0]
    )


def row_blocks(values, count):
    size = values.shape[0] // count
    return [values[i * size : (i + 1) * size] for i in range(count)]


def piece(values, index, count, axis):
    size = values.shape[axis] // count
    return lax.dynamic_slice_in_dim(values, index * size, size, axis)


def total_all(values):
    values = tree_sum(spread_row(values))
    values = tree_sum(spread_z(values))
    return values + swap_core(values)


def gelu_parts(gate):
    scale = math.sqrt(2.0 / math.pi)
    cube = 0.044715 * gate * gate * gate
    tanh = jnp.tanh(scale * (gate + cube))
    half = 0.5 * (1.0 + tanh)
    slope = half + 0.5 * gate * (1.0 - tanh * tanh) * scale * (1.0 + 3 * 0.044715 * gate * gate)
    return (gate * half, slope)


def norm_back(values, norm_gain, incoming):
    inverse = lax.rsqrt(jnp.mean(values * values, axis=1, keepdims=True) + EPSILON)
    scaled = incoming * norm_gain
    mean_product = jnp.mean(scaled * values, axis=1, keepdims=True)
    grad = inverse * scaled - values * (inverse * inverse * inverse) * mean_product
    return (grad, jnp.sum(incoming * values * inverse, axis=0))


def assemble(blocks, indices, axis, splits=None):
    height, breadth = blocks[0].shape
    splits = [breadth] if splits is None else splits
    count = len(blocks)

    def body(index_ref, *refs):
        block_refs, out_refs = refs[:count], refs[count:]
        for i in range(count):

            @pl.when(pl.program_id(0) == i)
            def _(i=i):
                at = 0
                for size, out_ref in zip(splits, out_refs):
                    out_ref[...] = block_refs[i][:, at : at + size]
                    at += size

    if axis == 0:
        shapes = [(height * count, size) for size in splits]
        out_specs = [pl.BlockSpec((height, size), lambda i, o: (o[i], 0)) for size in splits]
    else:
        shapes = [(height, breadth * count)]
        out_specs = [pl.BlockSpec((height, breadth), lambda i, o: (0, o[i]))]
    results = pl.pallas_call(
        body,
        grid_spec=pltpu.PrefetchScalarGridSpec(
            num_scalar_prefetch=1,
            grid=(count,),
            in_specs=[pl.BlockSpec((height, breadth), lambda i, o: (0, 0))] * count,
            out_specs=out_specs,
        ),
        out_shape=[jax.ShapeDtypeStruct(shape, blocks[0].dtype) for shape in shapes],
        name="assemble",
    )(jnp.stack(indices).astype(jnp.int32), *blocks)
    return results if len(results) > 1 else results[0]


def pack_units(order, flat, tall, half):
    rows = flat.shape[0]
    count = flat.shape[1] // (2 * half)

    def body(order_ref, gate_ref, up_ref, tall_ref, out_ref):
        out_ref[0] = gate_ref[...]
        out_ref[1] = up_ref[...]
        out_ref[2] = low(wide(tall_ref[...]).T)

    return pl.pallas_call(
        body,
        grid_spec=pltpu.PrefetchScalarGridSpec(
            num_scalar_prefetch=1,
            grid=(order.shape[0],),
            in_specs=[
                pl.BlockSpec((rows, half), lambda i, o: (0, o[i])),
                pl.BlockSpec((rows, half), lambda i, o: (0, count + o[i])),
                pl.BlockSpec((half, rows), lambda i, o: (o[i], 0)),
            ],
            out_specs=pl.BlockSpec((None, 3, rows, half), lambda i, o: (i, 0, 0, 0)),
        ),
        out_shape=jax.ShapeDtypeStruct((order.shape[0], 3, rows, half), jnp.bfloat16),
        name="pack_units",
    )(order, flat, flat, tall)


def join_units(order, blocks, rank_block):
    _, rows, half = blocks[0].shape
    rank = rank_block.shape[1]
    steps = len(blocks)
    more = rank // rows

    def body(order_ref, *refs):
        block_refs, rank_ref, out_refs = refs[:steps], refs[steps], refs[steps + 1 :]
        for i in range(steps):

            @pl.when(pl.program_id(0) == i)
            def _(i=i):
                for j in range(3):
                    out_refs[j][...] = block_refs[i][j]

        for i in range(more):

            @pl.when(pl.program_id(0) == steps + i)
            def _(i=i):
                for j in range(3):
                    out_refs[j][...] = rank_ref[j, i * rows : (i + 1) * rows, :]

    extended = rows * steps + rank
    return pl.pallas_call(
        body,
        grid_spec=pltpu.PrefetchScalarGridSpec(
            num_scalar_prefetch=1,
            grid=(steps + more,),
            in_specs=[pl.BlockSpec((3, rows, half), lambda i, o: (0, 0, 0))] * steps
            + [pl.BlockSpec((3, rank, half), lambda i, o: (0, 0, 0))],
            out_specs=[pl.BlockSpec((rows, half), lambda i, o: (o[i], 0))] * 3,
        ),
        out_shape=[jax.ShapeDtypeStruct((extended, half), jnp.bfloat16)] * 3,
        compiler_params=pltpu.CompilerParams(vmem_limit_bytes=56 * 1024 * 1024),
        name="join_units",
    )(order, *blocks, rank_block)


def pick_columns(places, grads, rows):
    half = grads[0].shape[1]
    count = places.shape[0]

    def body(place_ref, *refs):
        for j, grad_ref in enumerate(refs[:-1]):
            refs[-1][j] = grad_ref[...]

    return pl.pallas_call(
        body,
        grid_spec=pltpu.PrefetchScalarGridSpec(
            num_scalar_prefetch=1,
            grid=(count,),
            in_specs=[pl.BlockSpec((rows, half), lambda i, o: (o[i], 0))] * len(grads),
            out_specs=pl.BlockSpec((None, len(grads), rows, half), lambda i, o: (i, 0, 0, 0)),
        ),
        out_shape=jax.ShapeDtypeStruct((count, len(grads), rows, half), jnp.bfloat16),
        name="pick_columns",
    )(places, *grads)


def merge_columns(places, grads, arrived):
    count, parts, rows, half = arrived.shape

    def body(place_ref, *refs):
        arrived_ref, out_ref = refs[-2:]
        for j, grad_ref in enumerate(refs[:-2]):
            out_ref[j] = low(wide(grad_ref[...]) + wide(arrived_ref[j ^ 1]))

    whole = pl.BlockSpec((None, parts, rows, half), lambda i, o: (i, 0, 0, 0))
    return pl.pallas_call(
        body,
        grid_spec=pltpu.PrefetchScalarGridSpec(
            num_scalar_prefetch=1,
            grid=(count,),
            in_specs=[pl.BlockSpec((rows, half), lambda i, o: (o[i], 0))] * parts + [whole],
            out_specs=whole,
        ),
        out_shape=jax.ShapeDtypeStruct(arrived.shape, jnp.bfloat16),
        name="merge_columns",
    )(places, *grads, arrived)


def unpack_units(order, parts, specs, rows, half, count):
    def body(order_ref, gate_ref, up_ref, tall_ref, pair_out, tall_out):
        pair_out[:, 0, :] = wide(gate_ref[...])
        pair_out[:, 1, :] = wide(up_ref[...])
        tall_out[...] = wide(tall_ref[...]).T

    return pl.pallas_call(
        body,
        grid_spec=pltpu.PrefetchScalarGridSpec(
            num_scalar_prefetch=1,
            grid=(count,),
            in_specs=specs,
            out_specs=[
                pl.BlockSpec((rows, 2, half), lambda i, o: (0, 0, o[i])),
                pl.BlockSpec((half, rows), lambda i, o: (o[i], 0)),
            ],
        ),
        out_shape=[
            jax.ShapeDtypeStruct((rows, 2, half * count), jnp.float32),
            jax.ShapeDtypeStruct((half * count, rows), jnp.float32),
        ],
        name="unpack_units",
    )(order, *parts)


def chunk_inner(values, gradient, own, other, chunk, kept, total):
    size, extended = values.shape
    half = own[0].shape[1]
    tile = min(256, half)
    tiles = half // tile
    copying = total > size

    def body(*refs):
        x_ref, g_ref = refs[:2]
        own_refs, other_refs = refs[2:5], refs[5:8]
        refs = refs[8 + (8 if kept is not None else 0) :]
        act_refs, gate_refs, up_refs = refs[0:2], refs[2:4], refs[4:6]
        step = pl.program_id(0)

        def part(weights, h):
            gate = jnp.dot(x_ref[...], weights[0][...], preferred_element_type=jnp.float32)
            up = jnp.dot(x_ref[...], weights[1][...], preferred_element_type=jnp.float32)
            incoming = jnp.dot(g_ref[...], weights[2][...], preferred_element_type=jnp.float32)
            value, slope = gelu_parts(gate)
            act_refs[h][...] = low(value * up)
            gate_refs[h][...] = low(incoming * up * slope)
            up_refs[h][...] = low(incoming * value)

        @pl.when(step < tiles)
        def _():
            part(own_refs, 0)

        @pl.when(step >= tiles)
        def _():
            part(other_refs, 1)

        if copying:

            @pl.when(step == 0)
            def _():
                refs[6][...] = x_ref[...]
                refs[7][...] = g_ref[...]

    def own_map(t):
        return jnp.minimum(t, tiles - 1)

    def other_map(t):
        return jnp.maximum(t - tiles, 0)

    row_spec = pl.BlockSpec((size, extended), lambda t: (0, 0))
    in_specs = [row_spec, row_spec]
    in_specs += [pl.BlockSpec((extended, tile), lambda t: (0, own_map(t)))] * 3
    in_specs += [pl.BlockSpec((extended, tile), lambda t: (0, other_map(t)))] * 3
    operands = [values, gradient, *own, *other]
    aliases = {}
    if kept is not None:
        in_specs += [pl.BlockSpec(memory_space=pl.ANY)] * 8
        aliases = {8 + i: i for i in range(8)}
        operands += list(kept)
    at = chunk if copying else 0
    out_specs = [
        pl.BlockSpec((size, tile), lambda t: (at, own_map(t))),
        pl.BlockSpec((size, tile), lambda t: (at, other_map(t))),
    ] * 3
    out_shape = [jax.ShapeDtypeStruct((total, half), jnp.bfloat16)] * 6
    if copying:
        out_specs += [pl.BlockSpec((size, extended), lambda t: (at, 0))] * 2
        out_shape += [jax.ShapeDtypeStruct((total, extended), jnp.bfloat16)] * 2
    return pl.pallas_call(
        body,
        grid=(2 * tiles,),
        in_specs=in_specs,
        out_specs=out_specs,
        out_shape=out_shape,
        input_output_aliases=aliases,
        compiler_params=pltpu.CompilerParams(vmem_limit_bytes=56 * 1024 * 1024),
        name="chunk_inner",
    )(*operands)


def chunk_outer(kept, own, other, chunk, size):
    half = own[0].shape[1]
    extended = own[0].shape[0]
    tile = 256

    def body(*refs):
        acts, gates, ups = refs[0:2], refs[2:4], refs[4:6]
        weights = (refs[6:9], refs[9:12])
        result_ref, middle_ref = refs[12:]

        def back(left, right):
            return lax.dot_general(
                left[...], right[...], (((1,), (1,)), ((), ())), preferred_element_type=jnp.float32
            )

        result_ref[...] = low(back(acts[0], weights[0][2]) + back(acts[1], weights[1][2]))
        middle_ref[...] = low(
            back(gates[0], weights[0][0])
            + back(gates[1], weights[1][0])
            + back(ups[0], weights[0][1])
            + back(ups[1], weights[1][1])
        )

    return pl.pallas_call(
        body,
        grid=(extended // tile,),
        in_specs=[pl.BlockSpec((size, half), lambda n: (chunk, 0))] * 6
        + [pl.BlockSpec((tile, half), lambda n: (n, 0))] * 6,
        out_specs=[pl.BlockSpec((size, tile), lambda n: (0, n))] * 2,
        out_shape=[jax.ShapeDtypeStruct((size, extended), jnp.bfloat16)] * 2,
        compiler_params=pltpu.CompilerParams(vmem_limit_bytes=56 * 1024 * 1024),
        name="chunk_outer",
    )(*kept[:6], *own, *other)


def per_device(
    tokens,
    cotangent,
    permutation,
    lengths,
    attention_gain,
    query_projection_weight,
    key_value_weight,
    projection_adapter_first,
    query_adapter_second,
    key_value_second,
    output_projection_weight,
    output_adapter_first,
    output_adapter_second,
    hidden_gain,
    gate_up_weight,
    widen_adapter_first,
    widen_adapter_second,
    down_projection_weight,
    narrow_adapter_first,
    narrow_adapter_second,
):
    token_count = tokens.shape[0]
    width = tokens.shape[1]
    rows = lax.axis_size("row")
    cols = lax.axis_size("col")
    depth = cols // CORES
    row = lax.axis_index("row")
    col = lax.axis_index("col")
    layer = col // CORES
    core = col % CORES
    group_size = token_count * rows
    head_dim = key_value_weight.shape[1] // 2
    rank = projection_adapter_first.shape[1]
    slice_width = width // cols
    share = token_count // cols
    half = gate_up_weight.shape[2] // cols

    def by_column(blocks):
        others = [swap_core(b) for b in blocks]
        placed = []
        for d in range(depth):
            placed.append((blocks[d], (layer ^ d) * CORES + core))
            placed.append((others[d], (layer ^ d) * CORES + 1 - core))
        return placed

    def deal(values):
        return lax.all_to_all(
            values.reshape(cols, share, width), "col", split_axis=0, concat_axis=0, tiled=True
        ).reshape(token_count, width)

    def reduce_col(stacked):
        own = lax.dynamic_index_in_dim(stacked, core, 1, keepdims=False)
        other = lax.dynamic_index_in_dim(stacked, 1 - core, 1, keepdims=False)
        summed = low(wide(own) + wide(swap_core(other)))
        blocks = [
            lax.dynamic_index_in_dim(summed, layer ^ d, 0, keepdims=False) for d in range(depth)
        ]
        return scatter_z(blocks)

    targets = jnp.arange(cols, dtype=jnp.int32)[:, None]
    slot_ids = jnp.arange(share, dtype=jnp.int32)[None, :]
    packed = (targets * rows + row) * token_count + col * share + slot_ids
    sources = jnp.take(permutation, packed.reshape(-1)) - (row * cols + col) * token_count
    residual_stream = wide(deal(tokens[sources]))
    output_gradient_rows = deal(cotangent[sources])

    places = jnp.concatenate(
        [(row ^ d) * token_count + jnp.arange(token_count, dtype=jnp.int32) for d in range(rows)]
    )
    segment, positions = group_layout(lengths[0], places)
    cosine, sine_table = rotary_tables(positions, head_dim)
    allowed = (segment[:, None] == segment[None, :]) & (places[None, :] <= places[:, None])

    query_width = query_projection_weight.shape[1]
    shared_weights = jnp.concatenate(
        [key_value_weight, projection_adapter_first, widen_adapter_first], axis=1
    )
    shared_width = shared_weights.shape[1]
    mine = jnp.concatenate(
        [query_projection_weight, piece(shared_weights, row, rows, 1)], axis=1
    )
    placed = by_column(spread_z(mine))
    query_complete, shared_mine = assemble(
        [p[0] for p in placed],
        [p[1] for p in placed],
        0,
        [query_width, shared_width // rows],
    )
    shared_full = assemble(spread_row(shared_mine), [row ^ d for d in range(rows)], 1)
    key_value_complete = shared_full[:, : 2 * head_dim]
    projection_first_complete = shared_full[:, 2 * head_dim : 2 * head_dim + rank]
    widen_first_complete = shared_full[:, 2 * head_dim + rank :]
    placed = by_column(spread_z(output_projection_weight))
    output_blocks = [p[0] for p in placed]
    output_index = [p[1] for p in placed]
    for i in range(rank // slice_width):
        output_blocks.append(output_adapter_first[:, i * slice_width : (i + 1) * slice_width])
        output_index.append(jnp.int32(cols + i))
    output_extended = assemble(output_blocks, output_index, 1)

    flat_main = lax.optimization_barrier(gate_up_weight.reshape(slice_width, -1))
    flat_rank = lax.optimization_barrier(widen_adapter_second.reshape(rank, -1))

    def relative(step):
        return (col ^ step).astype(jnp.int32)

    own_units = pack_units(
        jnp.stack([relative(CORES * d) for d in range(depth)]),
        flat_main,
        down_projection_weight,
        half,
    )
    partner_units = swap_core(
        pack_units(
            jnp.stack([relative(CORES * d + 1) for d in range(depth)]),
            flat_main,
            down_projection_weight,
            half,
        )
    )
    rank_units = pack_units(relative(0)[None], flat_rank, narrow_adapter_first, half)
    own_units, partner_units, query_complete, output_extended = lax.optimization_barrier(
        (own_units, partner_units, query_complete, output_extended)
    )
    unit_blocks = []
    unit_places = []
    for d in range(depth):
        for k, units in enumerate((own_units, partner_units)):
            unit_blocks.append(swap_z(units[d], d) if d else units[d])
            unit_places.append(relative(CORES * d + k))
    unit_places += [jnp.int32(cols + i) for i in range(rank // slice_width)]
    own_weights = join_units(jnp.stack(unit_places), unit_blocks, rank_units[0])
    other_weights = [swap_core(w) for w in own_weights]

    attn_gain = wide(attention_gain)
    input_rows = jnp.concatenate(spread_row(low(normalize(residual_stream, attn_gain))))
    adapter_projection = low(matrix_product(input_rows, projection_first_complete))
    query_linear = matrix_product(input_rows, query_complete) + matrix_product(
        adapter_projection, query_adapter_second
    )
    key_value_linear = matrix_product(input_rows, key_value_complete) + matrix_product(
        adapter_projection, key_value_second
    )
    heads_local = query_width // head_dim
    query_scale = head_dim ** (-0.5)
    queries = low(
        rotate(
            query_linear.reshape(group_size, heads_local, head_dim),
            cosine[:, None, :],
            sine_table[:, None, :],
        )
        * query_scale
    )
    key_rows = low(rotate(key_value_linear[:, :head_dim], cosine, sine_table))
    value_rows = low(key_value_linear[:, head_dim:])
    head_queries = [queries[:, h, :] for h in range(heads_local)]
    head_probs = []
    mixed_list = []
    for query in head_queries:
        products = inner_column_count(query, key_rows)
        scores = jnp.where(allowed, products, MASKED)
        exponent = jnp.exp(scores - jnp.max(scores, axis=1, keepdims=True))
        probs = exponent / jnp.sum(exponent, axis=1, keepdims=True)
        head_probs.append(probs)
        mixed_list.append(low(matrix_product(low(probs), value_rows)))
    mixed = jnp.concatenate(mixed_list, axis=1)
    attention_sums = low(matrix_product(mixed, output_extended))
    attention_piece = scatter_row(row_blocks(attention_sums, rows))
    adapter_output = low(attention_piece[:, width:])
    hidden_state = (
        residual_stream
        + attention_piece[:, :width]
        + matrix_product(adapter_output, output_adapter_second)
    )
    ffn_gain = wide(hidden_gain)
    middle = low(normalize(hidden_state, ffn_gain))

    def stretch(values, factor_rows):
        return spread_wide(
            jnp.concatenate(spread_z(jnp.concatenate([values, factor_rows], axis=1)))
        )

    gradient_chunks = stretch(
        output_gradient_rows, low(inner_column_count(output_gradient_rows, narrow_adapter_second))
    )
    middle_chunks = stretch(middle, low(matrix_product(middle, widen_first_complete)))
    chunk_size = depth * token_count
    joined = rows <= 4
    total = rows * chunk_size if joined else chunk_size
    kept = None
    kept_list = []
    middle_blocks = []
    result_blocks = []
    for c in range(rows):
        kept = chunk_inner(
            middle_chunks[c],
            gradient_chunks[c],
            own_weights,
            other_weights,
            c,
            kept if joined else None,
            total,
        )
        kept_list.append(kept)
        result_block, middle_block = chunk_outer(
            kept, own_weights, other_weights, c if joined else 0, chunk_size
        )
        result_blocks.append(result_block)
        middle_blocks.append(middle_block)
    if joined:
        pieces = [kept]
    else:
        pieces = [
            [*k, m, g] for k, m, g in zip(kept_list, middle_chunks, gradient_chunks)
        ]
    middle_rows = scatter_row(middle_blocks)
    middle_rows, result_blocks = lax.optimization_barrier((middle_rows, result_blocks))
    middle_piece = scatter_z(row_blocks(middle_rows, depth))

    def core_sum(values):
        return wide(values) + wide(swap_core(values))

    def over_rows(left, right):
        parts = [inner_row_count(p[left], p[right]) for p in pieces]
        return sum(parts[1:], parts[0])

    grads = []
    for left, right in ((6, 2), (6, 4), (7, 0)):
        grads.append(low(over_rows(left, right)))
        grads.append(low(over_rows(left, right + 1)))
    parity = [(layer ^ d) * CORES for d in range(depth)]
    sent = pick_columns(
        jnp.stack([p + 1 - core for p in parity]).astype(jnp.int32), grads, slice_width
    )
    summed = merge_columns(
        jnp.stack([p + core for p in parity]).astype(jnp.int32), grads, swap_core(sent)
    )
    rank_grads = jnp.stack(
        [
            low(wide(grads[2 * j][width:]) + wide(swap_core(grads[2 * j + 1][width:])))
            for j in range(3)
        ]
    )
    summed, rank_grads, result_blocks, middle_piece = lax.optimization_barrier(
        (summed, rank_grads, result_blocks, middle_piece)
    )
    result_piece = scatter_z(row_blocks(scatter_row(result_blocks), depth))
    result_piece, hidden_again = lax.optimization_barrier((result_piece, hidden_state))
    adapter_final = low(result_piece[:, width:])
    block_result_rows = low(
        hidden_again
        + result_piece[:, :width]
        + matrix_product(adapter_final, narrow_adapter_second)
    )
    back_out = deal(block_result_rows)

    unit_stack = jnp.stack([summed[0]] + [swap_z(summed[d], d) for d in range(1, depth)])
    unit_order = jnp.stack([relative(e) for e in range(cols)])
    grad_expand_weight, grad_shrink_weight = unpack_units(
        unit_order,
        [unit_stack] * 3,
        [
            pl.BlockSpec(
                (None, None, slice_width, half),
                lambda i, o, j=j: (i // CORES, CORES * j + i % CORES, 0, 0),
            )
            for j in range(3)
        ],
        slice_width,
        half,
        cols,
    )
    rank_blocks = spread_z(rank_grads)
    rank_blocks = [b for block in rank_blocks for b in (block, swap_core(block))]
    rank_stack = jnp.stack(rank_blocks)
    widen_second_gradient, narrow_first_gradient = unpack_units(
        unit_order,
        [rank_stack] * 3,
        [
            pl.BlockSpec((None, None, rank, half), lambda i, o, j=j: (i, j, 0, 0))
            for j in range(3)
        ],
        rank,
        half,
        cols,
    )

    adapter_middle_gradient = low(middle_piece[:, width:])
    grad_normed_mid = middle_piece[:, :width] + inner_column_count(
        adapter_middle_gradient, widen_first_complete
    )
    grad_hidden_norm, grad_ffn_gain = norm_back(hidden_state, ffn_gain, grad_normed_mid)
    grad_hidden = wide(output_gradient_rows) + grad_hidden_norm
    attention_gradient = low(grad_hidden)

    final_all = jnp.concatenate(
        spread_row(
            jnp.concatenate(
                spread_z(jnp.concatenate([adapter_final, adapter_middle_gradient], axis=1))
            )
        )
    )

    def part_of(values, index, count):
        size = width // count
        return lax.dynamic_slice_in_dim(values, index * size, size, 1)

    def own_chunk(index):
        return final_all[index * chunk_size : (index + 1) * chunk_size] if not joined else final_all

    narrow_second_part = sum(
        inner_row_count(
            own_chunk(i)[:, :rank], part_of(p[7], row * depth + layer, rows * depth)
        )
        for i, p in enumerate(pieces)
    )
    narrow_second_part = low(core_sum(low(narrow_second_part)))
    narrow_second_gradient = wide(
        lax.all_gather(
            piece(narrow_second_part, core, CORES, 1), ("row", "col"), axis=1, tiled=True
        )
    )
    widen_first_part = low(
        sum(
            inner_row_count(
                piece(own_chunk(i)[:, rank:], row, rows, 1), part_of(p[6], layer, depth)
            )
            for i, p in enumerate(pieces)
        )
    )
    widen_first_part = low(
        wide(piece(widen_first_part, core, CORES, 1))
        + wide(swap_core(piece(widen_first_part, 1 - core, CORES, 1)))
    )
    widen_first_gradient = wide(jnp.concatenate(absolute(spread_row(widen_first_part), row))).T

    attention_rows = jnp.concatenate(spread_row(attention_gradient))
    attention_adapter_rows = low(inner_column_count(attention_rows, output_adapter_second))
    adapter_output_rows = jnp.concatenate(spread_row(adapter_output))
    grad_mixed = low(
        inner_column_count(
            jnp.concatenate([attention_rows, attention_adapter_rows], axis=1), output_extended
        )
    )
    output_part = low(inner_row_count(attention_rows, mixed))
    grad_output_weight = reduce_col(output_part.reshape(depth, CORES, slice_width, query_width)).T
    output_first_gradient, output_second_gradient = [
        wide(part)
        for part in lax.psum(
            (
                low(inner_row_count(mixed, attention_adapter_rows)),
                low(inner_row_count(adapter_output_rows, attention_rows)),
            ),
            "col",
        )
    ]

    grad_query_list = []
    grad_key_part = 0.0
    grad_value_part = 0.0
    for h in range(heads_local):
        grad_head = grad_mixed[:, h * head_dim : (h + 1) * head_dim]
        probs = head_probs[h]
        grad_probs = inner_column_count(grad_head, value_rows)
        shared = jnp.sum(probs * grad_probs, axis=1, keepdims=True)
        grad_scores = low(probs * (grad_probs - shared))
        grad_query_head = matrix_product(grad_scores, key_rows)
        grad_query_list.append(
            low(rotate(grad_query_head, cosine, -sine_table) * query_scale)
        )
        grad_key_part = grad_key_part + inner_row_count(grad_scores, head_queries[h])
        grad_value_part = grad_value_part + inner_row_count(low(probs), grad_head)
    query_gradient = jnp.concatenate(grad_query_list, axis=1)
    small_piece = scatter_row(
        row_blocks(
            jnp.concatenate(
                [
                    grad_key_part,
                    grad_value_part,
                    inner_column_count(query_gradient, query_adapter_second),
                ],
                axis=1,
            ),
            rows,
        )
    )
    own_cosine = cosine[:token_count]
    own_sine = sine_table[:token_count]
    own_key_value = low(
        jnp.concatenate(
            [
                rotate(small_piece[:, :head_dim], own_cosine, -own_sine),
                small_piece[:, head_dim : 2 * head_dim],
            ],
            axis=1,
        )
    )
    own_adapter = low(
        small_piece[:, 2 * head_dim :] + inner_column_count(own_key_value, key_value_second)
    )
    input_piece = scatter_row(row_blocks(inner_column_count(query_gradient, query_complete), rows))
    grad_normed_in = (
        input_piece
        + inner_column_count(own_key_value, key_value_complete)
        + inner_column_count(own_adapter, projection_first_complete)
    )
    grad_in_norm, grad_attn_gain = norm_back(residual_stream, attn_gain, grad_normed_in)
    back_grad = deal(low(grad_hidden + grad_in_norm))

    small_rows = jnp.concatenate(
        spread_row(jnp.concatenate([own_key_value, own_adapter], axis=1))
    )
    key_value_mine = piece(small_rows[:, : 2 * head_dim], row, rows, 1)
    adapter_mine = piece(small_rows[:, 2 * head_dim :], row, rows, 1)
    gradient_columns = jnp.concatenate([query_gradient, key_value_mine, adapter_mine], axis=1)
    input_part = low(inner_row_count(input_rows, gradient_columns))
    reduced = reduce_col(input_part.reshape(depth, CORES, slice_width, -1))
    grad_query_weight = reduced[:, :query_width]
    kv_width = 2 * head_dim // rows
    shared_blocks = absolute(spread_row(low(reduced[:, query_width:])), row)
    grad_keyval_weight = wide(jnp.concatenate([b[:, :kv_width] for b in shared_blocks], axis=1))
    projection_first_gradient = wide(
        jnp.concatenate([b[:, kv_width:] for b in shared_blocks], axis=1)
    )
    query_second_gradient, key_value_second_gradient = [
        wide(part)
        for part in lax.psum(
            (
                low(inner_row_count(adapter_projection, query_gradient)),
                low(inner_row_count(adapter_projection, small_rows[:, : 2 * head_dim])),
            ),
            "col",
        )
    ]

    gain_sums = total_all(jnp.stack([grad_attn_gain, grad_ffn_gain]))

    order = jnp.arange(token_count, dtype=jnp.int32)
    inverse = jnp.sum(
        jnp.where(sources[None, :] == order[:, None], order[None, :], 0), axis=1
    )
    return (
        back_out[inverse],
        back_grad[inverse],
        gain_sums[0],
        grad_query_weight,
        grad_keyval_weight,
        projection_first_gradient,
        query_second_gradient,
        key_value_second_gradient,
        grad_output_weight,
        output_first_gradient,
        output_second_gradient,
        gain_sums[1],
        grad_expand_weight,
        widen_first_gradient,
        widen_second_gradient,
        grad_shrink_weight,
        narrow_first_gradient,
        narrow_second_gradient,
    )


def solution(mesh):
    return jax.shard_map(
        per_device,
        mesh=mesh,
        in_specs=(
            P(("row", "col"), None),
            P(("row", "col"), None),
            P(),
            P("col", None),
            P(),
            P("col", "row"),
            P("col", None),
            P("col", None),
            P(None, "row"),
            P(),
            P("row", "col"),
            P("row", None),
            P(),
            P(),
            P("col", None, "row"),
            P("col", None),
            P(None, None, "row"),
            P("row", "col"),
            P("row", None),
            P(),
        ),
        out_specs=(
            P(("row", "col"), None),
            P(("row", "col"), None),
            P(),
            P("col", "row"),
            P("col", None),
            P("col", None),
            P(None, "row"),
            P(),
            P("row", "col"),
            P("row", None),
            P(),
            P(),
            P("col", None, "row"),
            P("col", None),
            P(None, None, "row"),
            P("row", "col"),
            P("row", None),
            P(),
        ),
        check_vma=False,
    )
```
